512 devices in a mesh: dp: 32 (over z, core), table: 16 (over x, y).
Axes of the slice: x: 4, y: 4, z: 16, core: 2. Of those that a mesh axis runs over, the one named last changes fastest.
Arguments:
- node_table: bfloat16 [1048576, 256], P(('dp', 'table')), may hold values from -6 to 6
- user_vectors: bfloat16 [131072, 256], P(('dp', 'table')), may hold values from -6 to 6
- first_weight: bfloat16 [768, 256], replicated, may hold values from -0.21875 to 0.21875
- first_bias: float32 [256], replicated, may hold values from -3 to 3
- second_weight: bfloat16 [256, 128], replicated, may hold values from -0.375 to 0.375
- second_bias: float32 [128], replicated, may hold values from -3 to 3
- out_weight: bfloat16 [128], replicated, may hold values from -0.5 to 0.5
- panel_rows: int32 [512, 512, 4], P(('dp', 'table')), may hold values from -1 to 2047, as said below
- pair_slots: int32 [131072, 8], P(('dp', 'table')), may hold values from 0 to 2047, as said below
Outputs:
- grad_table: float32 [1048576, 256], P(('dp', 'table'))
- grad_users: bfloat16 [131072, 256], P(('dp', 'table'))
The draws below stay inside these ranges and needn't reach their ends.
Inputs may be any that keep to these rules, and one draw needn't show every extreme that they name: panel_rows[d, o, j] is a row among owner o's 2048 rows (node o * 2048 + row) that device d's users visit, or -1 for an unused slot; the used slots of each d and o come first, 1 to 4 of them; every device uses all 4 slots on some owner, and some owners, the last one among them, have all 4 slots used by every device. pair_slots[u, k] = o * 4 + j names a used slot j of owner o in panel_rows[d, o] of the user's device d = u // 256; column 0 is the user's positive node, the others its beam negatives.
All inputs are finite; a program needn't handle non-finite values.
Results may differ from the reference program's by a relative error of at most 0.0052.
Values may be sent and summed in bfloat16 or wider, within the bound.
No kernel may reach another device: no remote copies, remote signals or barrier semaphores. Data moves between devices by JAX's collectives and lax.ppermute only.
A program may use at most 64 MiB of HBM per device.

```python
import jax
import jax.numpy as jnp
from jax import lax

W = 256
H1 = 256
H2 = 128
K = 8
CAP = 4
ROWS_DEV = 2048
U_DEV = 256
NODES = 1048576
USERS = 131072
DEVICES = 512


def visit_plan(key):
    first_key, second_key = jax.random.split(jax.random.fold_in(key, 11))
    offset = jax.random.randint(first_key, (), 0, 8)
    owners = jnp.arange(DEVICES, dtype=jnp.int32)
    hot_owner = ((owners + offset) % 8 == 0) | (owners == DEVICES - 1)
    base_count = 1 + jax.random.randint(second_key, (DEVICES, DEVICES), 0, CAP)
    return jnp.where(hot_owner[None, :], CAP, base_count).astype(jnp.int32)


def draw_panel_rows(key, part):
    counts = visit_plan(key)
    row_draw = jax.random.randint(jax.random.fold_in(key, 12), (DEVICES, DEVICES, CAP), 0, ROWS_DEV)
    slot_index = jnp.arange(CAP, dtype=jnp.int32)
    return jnp.where(slot_index[None, None, :] < counts[:, :, None], row_draw, -1).astype(jnp.int32)


def draw_pair_slots(key, part):
    counts = visit_plan(key)
    requester = (jnp.arange(USERS, dtype=jnp.int32) // U_DEV)[:, None]
    owners = jax.random.randint(jax.random.fold_in(key, 13), (USERS, K), 0, DEVICES)
    raw_pick = jax.random.randint(jax.random.fold_in(key, 14), (USERS, K), 0, 1 << 20)
    used = counts[requester, owners]
    slots = (owners * CAP + raw_pick % used).astype(jnp.int32)
    slots = slots.at[0, 1].set(0)
    slots = slots.at[USERS - 1, K - 1].set(DEVICES * CAP - 1)
    return slots.astype(jnp.int32)


def steps_of(rng, dims, shards, least, largest):
    def one(axis_at, blocks):
        heights = jax.random.uniform(jax.random.fold_in(jax.random.fold_in(rng, 6), axis_at), (blocks,), jnp.float32, least / len(shards), largest / len(shards))
        return jnp.repeat(jnp.exp(heights), dims[axis_at] // blocks).reshape((-1,) + (1,) * (len(dims) - axis_at - 1))

    level = one(*shards[0])
    for cut in shards[1:]:
        level = level * one(*cut)
    return level


def bell_draw(key, extent, spread, reach, pieces=(), kind=jnp.bfloat16):
    factor_of = steps_of(key, extent, pieces, -0.22, 0.18) if pieces else 1.0
    values = jax.random.normal(key, extent, jnp.float32) * spread * factor_of
    return jnp.minimum(jnp.maximum(values, -reach), reach).astype(kind)


def setup_inputs(seed: int = 0) -> dict:
    splits = jax.random.split(jax.random.key(seed), 10)
    return {
        "node_table": bell_draw(splits[0], (NODES, W), 1.0, 6.0, ((0, 512),)),
        "user_vectors": bell_draw(splits[1], (USERS, W), 1.0, 6.0, ((0, 512),)),
        "first_weight": bell_draw(splits[2], (3 * W, H1), (3 * W) ** -0.5, 0.21875),
        "first_bias": bell_draw(splits[3], (H1,), 0.5, 3.0, (), jnp.float32),
        "second_weight": bell_draw(splits[4], (H1, H2), H1 ** -0.5, 0.375),
        "second_bias": bell_draw(splits[5], (H2,), 0.5, 3.0, (), jnp.float32),
        "out_weight": bell_draw(splits[6], (H2,), H2 ** -0.5, 0.5),
        "panel_rows": draw_panel_rows(jax.random.fold_in(splits[9], 71), 0),
        "pair_slots": draw_pair_slots(jax.random.fold_in(splits[9], 71), 0),
    }


loss_scale = 32.0


def silu_slope(value):
    sig = jax.nn.sigmoid(value)
    return sig * (1.0 + value * (1.0 - sig))


def reference(node_table, user_vectors, first_weight, first_bias, second_weight, second_bias, out_weight, panel_rows, pair_slots):
    owners = pair_slots // CAP
    slot_index = pair_slots % CAP
    devices = (jnp.arange(USERS, dtype=jnp.int32) // U_DEV)[:, None]
    node_ids = (owners * ROWS_DEV + panel_rows[devices, owners, slot_index]).astype(jnp.int32)
    labels = (jnp.arange(K) == 0).astype(jnp.float32)

    def per_device(accum_table, block_data):
        user_rows, block_nodes = block_data
        flat_nodes = block_nodes.reshape(-1)
        item_vecs = node_table[flat_nodes].reshape(U_DEV, K, W)
        user_wide = jnp.broadcast_to(user_rows[:, None, :], (U_DEV, K, W))
        crossed = (user_wide.astype(jnp.float32) * item_vecs.astype(jnp.float32)).astype(jnp.bfloat16)
        joined = jnp.concatenate([user_wide, item_vecs, crossed], axis=2).reshape(U_DEV * K, 3 * W)
        pre_first = jnp.dot(joined, first_weight, preferred_element_type=jnp.float32) + first_bias
        hid_first = jax.nn.silu(pre_first).astype(jnp.bfloat16)
        pre_second = jnp.dot(hid_first, second_weight, preferred_element_type=jnp.float32) + second_bias
        hid_second = jax.nn.silu(pre_second).astype(jnp.bfloat16)
        logits = jnp.dot(hid_second, out_weight, preferred_element_type=jnp.float32)
        targets = jnp.tile(labels, U_DEV)
        logit_grad = loss_scale * (jax.nn.sigmoid(logits) - targets)
        delta_second = (logit_grad[:, None] * out_weight.astype(jnp.float32)[None, :] * silu_slope(pre_second)).astype(jnp.bfloat16)
        delta_first = (jnp.dot(delta_second, second_weight.T, preferred_element_type=jnp.float32) * silu_slope(pre_first)).astype(jnp.bfloat16)
        backward = jnp.dot(delta_first, first_weight.T, preferred_element_type=jnp.float32).reshape(U_DEV, K, 3 * W)
        user_f32 = user_rows.astype(jnp.float32)[:, None, :]
        item_f32 = item_vecs.astype(jnp.float32)
        grad_items = backward[:, :, W:2 * W] + backward[:, :, 2 * W:] * user_f32
        grad_users = jnp.sum(backward[:, :, :W] + backward[:, :, 2 * W:] * item_f32, axis=1).astype(jnp.bfloat16)
        accum_table = accum_table.at[flat_nodes].add(grad_items.reshape(U_DEV * K, W))
        return accum_table, grad_users

    start_table = jnp.zeros((NODES, W), jnp.float32)
    grad_table, grad_users = lax.scan(per_device, start_table, (user_vectors.reshape(DEVICES, U_DEV, W), node_ids.reshape(DEVICES, U_DEV, K)))
    return grad_table, grad_users.reshape(USERS, W)
```

```python
import jax
import jax.numpy as jnp
from jax import lax
from jax.experimental import pallas as pl
from jax.experimental.pallas import tpu as pltpu
from jax.sharding import PartitionSpec as P

loss_scale = 32.0
BOTH = ("dp", "table")
ROW_BLOCK = 512


def slope_of(value, sig):
    return sig * (1.0 + value * (1.0 - sig))


def pick_kernel(index_ref, table_ref, out_ref):
    rows = table_ref.shape[0]
    table = table_ref[...]
    columns = index_ref[...].T
    per_block = ROW_BLOCK // 128
    for block in range(out_ref.shape[0] // ROW_BLOCK):
        hot = []
        for part in range(per_block):
            at = block * per_block + part
            wanted = columns[:, at : at + 1]
            hot.append(wanted == lax.broadcasted_iota(jnp.int32, (128, rows), 1))
        hot = jnp.concatenate([one.astype(jnp.float32) for one in hot], axis=0).astype(jnp.bfloat16)
        out_ref[block * ROW_BLOCK : (block + 1) * ROW_BLOCK, :] = jnp.dot(
            hot, table, preferred_element_type=jnp.float32
        ).astype(out_ref.dtype)


def pick_rows(index, table):
    count = index.size
    return pl.pallas_call(
        pick_kernel,
        out_shape=jax.ShapeDtypeStruct((count, table.shape[1]), table.dtype),
        in_specs=[pl.BlockSpec(memory_space=pltpu.VMEM)] * 2,
        out_specs=pl.BlockSpec(memory_space=pltpu.VMEM),
        name="pick_rows",
    )(index.reshape(count // 128, 128), table)


def sum_block(index_row, first, values):
    count = index_row.shape[1]
    row_id = lax.broadcasted_iota(jnp.int32, (ROW_BLOCK, count), 0) + first
    hot = (row_id == index_row).astype(jnp.float32).astype(jnp.bfloat16)
    return jnp.dot(hot, values, preferred_element_type=jnp.float32)


def sum_kernel(index_ref, value_ref, out_ref):
    first = pl.program_id(0) * ROW_BLOCK
    out_ref[...] = sum_block(index_ref[...], first, value_ref[...])


def sum_rows(index_row, values, rows):
    count, width = values.shape
    return pl.pallas_call(
        sum_kernel,
        out_shape=jax.ShapeDtypeStruct((rows, width), jnp.float32),
        grid=(rows // ROW_BLOCK,),
        in_specs=[
            pl.BlockSpec((1, count), lambda i: (0, 0)),
            pl.BlockSpec((count, width), lambda i: (0, 0)),
        ],
        out_specs=pl.BlockSpec((ROW_BLOCK, width), lambda i: (i, 0)),
        name="sum_rows",
    )(index_row, values)


def contract_last(left, right):
    return lax.dot_general(left, right, (((1,), (1,)), ((), ())), preferred_element_type=jnp.float32)


def scorer_kernel(
    column_ref,
    row_ref,
    panel_ref,
    user_ref,
    first_ref,
    bias_one_ref,
    second_ref,
    bias_two_ref,
    last_ref,
    slot_ref,
    user_out_ref,
    user_part,
    user_sum,
    item_grads,
):
    step = pl.program_id(0)
    users, width = user_ref.shape
    slots = panel_ref.shape[0]
    user = user_ref[...]
    user_wide = user.astype(jnp.float32)

    @pl.when(step == 0)
    def _():
        user_part[...] = (
            jnp.dot(user, first_ref[:width, :], preferred_element_type=jnp.float32)
            + bias_one_ref[...]
        )
        user_sum[...] = jnp.zeros_like(user_sum)

    hot = column_ref[0] == lax.broadcasted_iota(jnp.int32, (users, slots), 1)
    item_wide = jnp.dot(
        hot.astype(jnp.float32).astype(jnp.bfloat16),
        panel_ref[...],
        preferred_element_type=jnp.float32,
    )
    item = item_wide.astype(jnp.bfloat16)
    crossed = (user_wide * item_wide).astype(jnp.bfloat16)
    pre_one = (
        jnp.dot(item, first_ref[width : 2 * width, :], preferred_element_type=jnp.float32)
        + jnp.dot(crossed, first_ref[2 * width :, :], preferred_element_type=jnp.float32)
        + user_part[...]
    )
    sig_one = jax.nn.sigmoid(pre_one)
    hid_one = (pre_one * sig_one).astype(jnp.bfloat16)
    second = second_ref[...]
    pre_two = jnp.dot(hid_one, second, preferred_element_type=jnp.float32) + bias_two_ref[...]
    sig_two = jax.nn.sigmoid(pre_two)
    hid_two = (pre_two * sig_two).astype(jnp.bfloat16)
    last = last_ref[...].astype(jnp.float32)
    logits = jnp.sum(hid_two.astype(jnp.float32) * last, axis=1, keepdims=True)
    target = jnp.where(step == 0, 1.0, 0.0)
    logit_grad = loss_scale * (jax.nn.sigmoid(logits) - target)
    delta_two = (logit_grad * last * slope_of(pre_two, sig_two)).astype(jnp.bfloat16)
    delta_one = (contract_last(delta_two, second) * slope_of(pre_one, sig_one)).astype(jnp.bfloat16)
    back_cross = contract_last(delta_one, first_ref[2 * width :, :])
    grads = contract_last(delta_one, first_ref[width : 2 * width, :]) + back_cross * user_wide
    item_grads[pl.ds(pl.multiple_of(step * users, users), users), :] = grads.astype(jnp.bfloat16)
    user_sum[...] += contract_last(delta_one, first_ref[:width, :]) + back_cross * item_wide

    @pl.when(step == pl.num_programs(0) - 1)
    def _():
        user_out_ref[...] = user_sum[...].astype(user_out_ref.dtype)
        index_row = row_ref[...]
        values = item_grads[...]
        for block in range(slots // ROW_BLOCK):
            first = block * ROW_BLOCK
            slot_ref[first : first + ROW_BLOCK, :] = sum_block(index_row, first, values).astype(
                slot_ref.dtype
            )


def run_scorer(pair_slots, panels, users, first_weight, first_bias, second_weight, second_bias, out_weight):
    user_count, per_user = pair_slots.shape
    slots, width = panels.shape
    by_column = pair_slots.T
    hidden_one, hidden_two = second_weight.shape
    whole = lambda *shape: pl.BlockSpec(shape, lambda i: (0,) * len(shape))
    return pl.pallas_call(
        scorer_kernel,
        out_shape=(
            jax.ShapeDtypeStruct((slots, width), jnp.bfloat16),
            jax.ShapeDtypeStruct((user_count, width), jnp.bfloat16),
        ),
        grid=(per_user,),
        in_specs=[
            pl.BlockSpec((1, user_count, 1), lambda i: (i, 0, 0)),
            whole(1, user_count * per_user),
            whole(slots, width),
            whole(user_count, width),
            whole(3 * width, hidden_one),
            whole(1, hidden_one),
            whole(hidden_one, hidden_two),
            whole(1, hidden_two),
            whole(1, hidden_two),
        ],
        out_specs=(whole(slots, width), whole(user_count, width)),
        scratch_shapes=[
            pltpu.VMEM((user_count, hidden_one), jnp.float32),
            pltpu.VMEM((user_count, width), jnp.float32),
            pltpu.VMEM((user_count * per_user, width), jnp.bfloat16),
        ],
        name="run_scorer",
    )(
        by_column.reshape(per_user, user_count, 1),
        by_column.reshape(1, user_count * per_user),
        panels,
        users,
        first_weight,
        first_bias.reshape(1, -1),
        second_weight,
        second_bias.reshape(1, -1),
        out_weight.reshape(1, -1),
    )


def swap(blocks, axis):
    return lax.all_to_all(blocks, axis, split_axis=0, concat_axis=0, tiled=True)


def swap_rows(rows, count):
    width = rows.shape[1]
    return swap(rows.reshape(count, -1, width), BOTH).reshape(-1, width)


def body(
    node_table,
    user_vectors,
    first_weight,
    first_bias,
    second_weight,
    second_bias,
    out_weight,
    panel_rows,
    pair_slots,
):
    count_dp = lax.axis_size("dp")
    count_table = lax.axis_size("table")
    count = count_dp * count_table
    slot_cap = panel_rows.shape[2]
    wanted = panel_rows.reshape(count_dp, count_table, slot_cap).transpose(1, 0, 2)
    wanted = swap(wanted.reshape(count_table, count_dp * slot_cap), "table")
    wanted = wanted.reshape(count_table, count_dp, slot_cap).transpose(1, 0, 2)
    requested = swap(wanted.reshape(count_dp, count_table * slot_cap), "dp").reshape(-1)
    picked = pick_rows(requested, node_table)
    panels = swap_rows(picked, count)
    slot_grads, user_grads = run_scorer(
        pair_slots,
        panels,
        user_vectors,
        first_weight,
        first_bias,
        second_weight,
        second_bias,
        out_weight,
    )
    returned = swap_rows(slot_grads, count)
    grad_table = sum_rows(requested.reshape(1, -1), returned, node_table.shape[0])
    return (grad_table, user_grads)


def solution(mesh):
    placed = (
        P(BOTH, None),
        P(BOTH, None),
        P(),
        P(),
        P(),
        P(),
        P(),
        P(BOTH, None, None),
        P(BOTH, None),
    )
    return jax.shard_map(
        body,
        mesh=mesh,
        in_specs=placed,
        out_specs=(P(BOTH, None), P(BOTH, None)),
        check_vma=False,
    )
```

```python
import jax
import jax.numpy as jnp
from jax import lax
from jax.experimental import pallas as pl
from jax.experimental.pallas import tpu as pltpu
from jax.sharding import PartitionSpec as P

loss_scale = 32.0
BOTH = ("dp", "table")
ROW_BLOCK = 512
PAIR_BLOCK = 512
PICK_BLOCK = 512


def slope_of(value, sig):
    return sig * (1.0 + value * (1.0 - sig))


def contract_last(left, right):
    return lax.dot_general(left, right, (((1,), (1,)), ((), ())), preferred_element_type=jnp.float32)


def low_half(rows):
    return lax.broadcasted_iota(jnp.int32, (rows, 8, 128), 1) < 4


def to_tiles(rows):
    groups = rows.shape[0] // 8
    parts = rows.reshape(groups, 8, 256)
    left, right = parts[:, :, :128], parts[:, :, 128:]
    low = low_half(groups)
    even = jnp.where(low, left, pltpu.roll(right, 4, 1))
    odd = jnp.where(low, pltpu.roll(left, 4, 1), right)
    return even, odd


def from_tiles(even, odd):
    groups = even.shape[0]
    low = low_half(groups)
    left = jnp.where(low, even, pltpu.roll(odd, 4, 1))
    right = jnp.where(low, pltpu.roll(even, 4, 1), odd)
    return left.reshape(groups * 8, 128), right.reshape(groups * 8, 128)


def unpack_tiles(tile_ref, out_ref):
    block = 64
    for first in range(0, tile_ref.shape[0], block):
        even = tile_ref[first : first + block, 0].astype(jnp.float32)
        odd = tile_ref[first : first + block, 1].astype(jnp.float32)
        left, right = from_tiles(even, odd)
        out_ref[8 * first : 8 * (first + block), :128] = left.astype(out_ref.dtype)
        out_ref[8 * first : 8 * (first + block), 128:] = right.astype(out_ref.dtype)


def store_tiles(rows, first, out_ref):
    even, odd = to_tiles(rows)
    at = first // 8
    out_ref[at : at + even.shape[0], 0] = even.astype(out_ref.dtype)
    out_ref[at : at + even.shape[0], 1] = odd.astype(out_ref.dtype)


def pick_block(columns, first, count, table):
    part = columns.shape[0]
    hot = []
    for at in range(first // part, (first + count) // part):
        ids = lax.broadcasted_iota(jnp.int32, (part, table.shape[0]), 1)
        hot.append((columns[:, at : at + 1] == ids).astype(jnp.float32).astype(jnp.bfloat16))
    return jnp.dot(jnp.concatenate(hot, axis=0), table, preferred_element_type=jnp.float32)


def sum_block(index_row, first, values):
    count = index_row.shape[1]
    row_id = lax.broadcasted_iota(jnp.int32, (ROW_BLOCK, count), 0) + first
    hot = (row_id == index_row).astype(jnp.float32).astype(jnp.bfloat16)
    return jnp.dot(hot, values, preferred_element_type=jnp.float32)


VMEM = pl.BlockSpec(memory_space=pltpu.VMEM)


def pick_kernel(index_ref, table_ref, out_ref):
    table = table_ref[...]
    columns = index_ref[...].T
    for first in range(0, index_ref.size, PICK_BLOCK):
        store_tiles(pick_block(columns, first, PICK_BLOCK, table), first, out_ref)


def pick_rows(index, table):
    return pl.pallas_call(
        pick_kernel,
        out_shape=jax.ShapeDtypeStruct((index.size // 8, 2, 8, 128), table.dtype),
        in_specs=[VMEM] * 2,
        out_specs=VMEM,
        name="pick_rows",
        compiler_params=pltpu.CompilerParams(vmem_limit_bytes=24 << 20),
    )(index.reshape(-1, 64), table)


def sum_kernel(index_ref, tile_ref, out_ref, values):
    @pl.when(pl.program_id(0) == 0)
    def _():
        unpack_tiles(tile_ref, values)

    first = pl.program_id(0) * ROW_BLOCK
    out_ref[...] = sum_block(index_ref[...], first, values[...])


def sum_rows(index_row, tiles, rows):
    count = index_row.shape[1]
    return pl.pallas_call(
        sum_kernel,
        out_shape=jax.ShapeDtypeStruct((rows, 256), jnp.float32),
        grid=(rows // ROW_BLOCK,),
        in_specs=[
            pl.BlockSpec((1, count), lambda i: (0, 0)),
            pl.BlockSpec(tiles.shape, lambda i: (0, 0, 0, 0)),
        ],
        out_specs=pl.BlockSpec((ROW_BLOCK, 256), lambda i: (i, 0)),
        scratch_shapes=[pltpu.VMEM((count, 256), tiles.dtype)],
        name="sum_rows",
        compiler_params=pltpu.CompilerParams(vmem_limit_bytes=24 << 20),
    )(index_row, tiles)


def scorer_kernel(
    index_ref,
    row_ref,
    tile_ref,
    user_ref,
    first_ref,
    bias_one_ref,
    second_ref,
    bias_two_ref,
    last_ref,
    slot_ref,
    user_out_ref,
    panel_ref,
    item_grads,
):
    users, width = user_ref.shape
    pairs = index_ref.size
    slots = panel_ref.shape[0]
    unpack_tiles(tile_ref, panel_ref)
    panels = panel_ref[...]
    columns = index_ref[...].T
    user = user_ref[...]
    last = last_ref[...].astype(jnp.float32)
    second = second_ref[...]
    weight_user = first_ref[:width, :]
    weight_item = first_ref[width : 2 * width, :]
    weight_cross = first_ref[2 * width :, :]
    repeat = PAIR_BLOCK // users
    user_wide = jnp.concatenate([user.astype(jnp.float32)] * repeat, axis=0)
    user_part = jnp.dot(user, weight_user, preferred_element_type=jnp.float32) + bias_one_ref[...]
    user_part = jnp.concatenate([user_part] * repeat, axis=0)

    def fold(block):
        total = block[:users]
        for at in range(1, repeat):
            total = total + block[at * users : (at + 1) * users]
        return total

    delta_sum = jnp.zeros((users, width), jnp.float32)
    cross_sum = jnp.zeros((users, width), jnp.float32)
    ahead = pick_block(columns, 0, PAIR_BLOCK, panels)
    for first in range(0, pairs, PAIR_BLOCK):
        item_wide = ahead
        if first + PAIR_BLOCK < pairs:
            ahead = pick_block(columns, first + PAIR_BLOCK, PAIR_BLOCK, panels)
        item = item_wide.astype(jnp.bfloat16)
        crossed = (user_wide * item_wide).astype(jnp.bfloat16)
        pre_one = (
            jnp.dot(item, weight_item, preferred_element_type=jnp.float32)
            + jnp.dot(crossed, weight_cross, preferred_element_type=jnp.float32)
            + user_part
        )
        sig_one = jax.nn.sigmoid(pre_one)
        hid_one = (pre_one * sig_one).astype(jnp.bfloat16)
        pre_two = jnp.dot(hid_one, second, preferred_element_type=jnp.float32) + bias_two_ref[...]
        sig_two = jax.nn.sigmoid(pre_two)
        hid_two = (pre_two * sig_two).astype(jnp.bfloat16)
        logits = jnp.sum(hid_two.astype(jnp.float32) * last, axis=1, keepdims=True)
        logit_grad = jax.nn.sigmoid(logits)
        if first == 0:
            place = lax.broadcasted_iota(jnp.int32, logits.shape, 0)
            logit_grad = logit_grad - jnp.where(place < users, 1.0, 0.0)
        logit_grad = loss_scale * logit_grad
        delta_two = (logit_grad * last * slope_of(pre_two, sig_two)).astype(jnp.bfloat16)
        delta_one = contract_last(delta_two, second) * slope_of(pre_one, sig_one)
        delta_one = delta_one.astype(jnp.bfloat16)
        back_cross = contract_last(delta_one, weight_cross)
        grads = contract_last(delta_one, weight_item) + back_cross * user_wide
        item_grads[first : first + PAIR_BLOCK, :] = grads.astype(jnp.bfloat16)
        delta_sum = delta_sum + fold(delta_one.astype(jnp.float32))
        cross_sum = cross_sum + fold(back_cross * item_wide)
    delta_high = delta_sum.astype(jnp.bfloat16)
    delta_low = (delta_sum - delta_high.astype(jnp.float32)).astype(jnp.bfloat16)
    user_grads = contract_last(delta_high, weight_user) + contract_last(delta_low, weight_user)
    user_out_ref[...] = (user_grads + cross_sum).astype(user_out_ref.dtype)
    index_row = row_ref[...]
    values = item_grads[...]
    for first in range(0, slots, ROW_BLOCK):
        store_tiles(sum_block(index_row, first, values), first, slot_ref)


def run_scorer(pair_slots, tiles, users, first_weight, first_bias, second_weight, second_bias, out_weight):
    pairs = pair_slots.size
    width = users.shape[1]
    by_column = pair_slots.T
    return pl.pallas_call(
        scorer_kernel,
        out_shape=(
            jax.ShapeDtypeStruct(tiles.shape, jnp.bfloat16),
            jax.ShapeDtypeStruct(users.shape, jnp.bfloat16),
        ),
        in_specs=[VMEM] * 9,
        out_specs=(VMEM, VMEM),
        scratch_shapes=[
            pltpu.VMEM((tiles.size // width, width), jnp.bfloat16),
            pltpu.VMEM((pairs, width), jnp.bfloat16),
        ],
        name="run_scorer",
        compiler_params=pltpu.CompilerParams(vmem_limit_bytes=24 << 20),
    )(
        by_column.reshape(pairs // 128, 128),
        by_column.reshape(1, pairs),
        tiles,
        users,
        first_weight,
        first_bias.reshape(1, -1),
        second_weight,
        second_bias.reshape(1, -1),
        out_weight.reshape(1, -1),
    )


def swap(blocks, axis):
    return lax.all_to_all(blocks, axis, split_axis=0, concat_axis=0, tiled=True)


def swap_tiles(tiles, count):
    return swap(tiles.reshape(count, -1, 128), BOTH).reshape(tiles.shape)


def body(
    node_table,
    user_vectors,
    first_weight,
    first_bias,
    second_weight,
    second_bias,
    out_weight,
    panel_rows,
    pair_slots,
):
    count_dp = lax.axis_size("dp")
    count_table = lax.axis_size("table")
    count = count_dp * count_table
    slot_cap = panel_rows.shape[2]
    wanted = panel_rows.reshape(count_dp, count_table, slot_cap).transpose(1, 0, 2)
    wanted = swap(wanted.reshape(count_table, count_dp * slot_cap), "table")
    wanted = wanted.reshape(count_table, count_dp, slot_cap).transpose(1, 0, 2)
    requested = swap(wanted.reshape(count_dp, count_table * slot_cap), "dp")
    panels = swap_tiles(pick_rows(requested, node_table), count)
    slot_grads, user_grads = run_scorer(
        pair_slots,
        panels,
        user_vectors,
        first_weight,
        first_bias,
        second_weight,
        second_bias,
        out_weight,
    )
    returned = swap_tiles(slot_grads, count)
    grad_table = sum_rows(requested.reshape(1, -1), returned, node_table.shape[0])
    return (grad_table, user_grads)


def solution(mesh):
    placed = (
        P(BOTH, None),
        P(BOTH, None),
        P(),
        P(),
        P(),
        P(),
        P(),
        P(BOTH, None, None),
        P(BOTH, None),
    )
    return jax.shard_map(
        body,
        mesh=mesh,
        in_specs=placed,
        out_specs=(P(BOTH, None), P(BOTH, None)),
        check_vma=False,
    )
```

```python
import jax
import jax.numpy as jnp
from jax import lax
from jax.experimental import pallas as pl
from jax.experimental.pallas import tpu as pltpu
from jax.sharding import PartitionSpec as P

loss_scale = 32.0
BOTH = ("dp", "table")
ROW_BLOCK = 512
PAIR_BLOCK = 512
PICK_BLOCK = 512


def slope_of(value, sig):
    return sig * (1.0 + value * (1.0 - sig))


def contract_last(left, right):
    return lax.dot_general(left, right, (((1,), (1,)), ((), ())), preferred_element_type=jnp.float32)


def low_half(rows):
    return lax.broadcasted_iota(jnp.int32, (rows, 8, 128), 1) < 4


def to_tiles(rows):
    groups = rows.shape[0] // 8
    parts = rows.reshape(groups, 8, 256)
    left, right = parts[:, :, :128], parts[:, :, 128:]
    low = low_half(groups)
    even = jnp.where(low, left, pltpu.roll(right, 4, 1))
    odd = jnp.where(low, pltpu.roll(left, 4, 1), right)
    return even, odd


def from_tiles(even, odd):
    groups = even.shape[0]
    low = low_half(groups)
    left = jnp.where(low, even, pltpu.roll(odd, 4, 1))
    right = jnp.where(low, pltpu.roll(even, 4, 1), odd)
    return left.reshape(groups * 8, 128), right.reshape(groups * 8, 128)


def unpack_tiles(tile_ref, out_ref):
    block = 64
    for first in range(0, tile_ref.shape[0], block):
        even = tile_ref[first : first + block, 0].astype(jnp.float32)
        odd = tile_ref[first : first + block, 1].astype(jnp.float32)
        left, right = from_tiles(even, odd)
        out_ref[8 * first : 8 * (first + block), :128] = left.astype(out_ref.dtype)
        out_ref[8 * first : 8 * (first + block), 128:] = right.astype(out_ref.dtype)


def store_tiles(rows, first, out_ref):
    even, odd = to_tiles(rows)
    at = first // 8
    out_ref[at : at + even.shape[0], 0] = even.astype(out_ref.dtype)
    out_ref[at : at + even.shape[0], 1] = odd.astype(out_ref.dtype)


def pick_block(columns, first, count, table):
    part = columns.shape[0]
    hot = []
    for at in range(first // part, (first + count) // part):
        ids = lax.broadcasted_iota(jnp.int32, (part, table.shape[0]), 1)
        hot.append((columns[:, at : at + 1] == ids).astype(jnp.float32).astype(jnp.bfloat16))
    return jnp.dot(jnp.concatenate(hot, axis=0), table, preferred_element_type=jnp.float32)


def sum_block(index_row, first, values):
    count = index_row.shape[1]
    row_id = lax.broadcasted_iota(jnp.int32, (ROW_BLOCK, count), 0) + first
    hot = (row_id == index_row).astype(jnp.float32).astype(jnp.bfloat16)
    return jnp.dot(hot, values, preferred_element_type=jnp.float32)


VMEM = pl.BlockSpec(memory_space=pltpu.VMEM)


def pick_kernel(index_ref, table_ref, out_ref):
    table = table_ref[...]
    columns = index_ref[...].T
    for first in range(0, index_ref.size, PICK_BLOCK):
        store_tiles(pick_block(columns, first, PICK_BLOCK, table), first, out_ref)


def stage_kernel(table_ref, out_ref):
    out_ref[...] = table_ref[...]


def stage_table(table):
    return pl.pallas_call(
        stage_kernel,
        out_shape=jax.ShapeDtypeStruct(table.shape, table.dtype),
        in_specs=[VMEM],
        out_specs=VMEM,
        name="stage_table",
        compiler_params=pltpu.CompilerParams(vmem_limit_bytes=8 << 20),
        cost_estimate=pl.CostEstimate(flops=0, bytes_accessed=2 * table.size * 2, transcendentals=0),
    )(table)


def pick_rows(index, table):
    return pl.pallas_call(
        pick_kernel,
        out_shape=jax.ShapeDtypeStruct((index.size // 8, 2, 8, 128), table.dtype),
        in_specs=[VMEM] * 2,
        out_specs=VMEM,
        name="pick_rows",
        compiler_params=pltpu.CompilerParams(vmem_limit_bytes=24 << 20),
    )(index.reshape(-1, 64), table)


def sum_kernel(index_ref, tile_ref, out_ref, values):
    @pl.when(pl.program_id(0) == 0)
    def _():
        unpack_tiles(tile_ref, values)

    first = pl.program_id(0) * ROW_BLOCK
    out_ref[...] = sum_block(index_ref[...], first, values[...])


def sum_rows(index_row, tiles, rows):
    count = index_row.shape[1]
    return pl.pallas_call(
        sum_kernel,
        out_shape=jax.ShapeDtypeStruct((rows, 256), jnp.float32),
        grid=(rows // ROW_BLOCK,),
        in_specs=[
            pl.BlockSpec((1, count), lambda i: (0, 0)),
            pl.BlockSpec(tiles.shape, lambda i: (0, 0, 0, 0)),
        ],
        out_specs=pl.BlockSpec((ROW_BLOCK, 256), lambda i: (i, 0)),
        scratch_shapes=[pltpu.VMEM((count, 256), tiles.dtype)],
        name="sum_rows",
        compiler_params=pltpu.CompilerParams(vmem_limit_bytes=24 << 20),
    )(index_row, tiles)


def scorer_kernel(
    index_ref,
    row_ref,
    tile_ref,
    user_ref,
    first_ref,
    bias_one_ref,
    second_ref,
    bias_two_ref,
    last_ref,
    slot_ref,
    user_out_ref,
    panel_ref,
    item_grads,
):
    users, width = user_ref.shape
    pairs = index_ref.size
    slots = panel_ref.shape[0]
    unpack_tiles(tile_ref, panel_ref)
    panels = panel_ref[...]
    columns = index_ref[...].T
    user = user_ref[...]
    last = last_ref[...].astype(jnp.float32)
    second = second_ref[...]
    weight_user = first_ref[:width, :]
    weight_item = first_ref[width : 2 * width, :]
    weight_cross = first_ref[2 * width :, :]
    repeat = PAIR_BLOCK // users
    user_wide = jnp.concatenate([user.astype(jnp.float32)] * repeat, axis=0)
    user_part = jnp.dot(user, weight_user, preferred_element_type=jnp.float32) + bias_one_ref[...]
    user_part = jnp.concatenate([user_part] * repeat, axis=0)

    def fold(block):
        total = block[:users]
        for at in range(1, repeat):
            total = total + block[at * users : (at + 1) * users]
        return total

    delta_sum = jnp.zeros((users, width), jnp.float32)
    cross_sum = jnp.zeros((users, width), jnp.float32)
    ahead = pick_block(columns, 0, PAIR_BLOCK, panels)
    for first in range(0, pairs, PAIR_BLOCK):
        item_wide = ahead
        if first + PAIR_BLOCK < pairs:
            ahead = pick_block(columns, first + PAIR_BLOCK, PAIR_BLOCK, panels)
        item = item_wide.astype(jnp.bfloat16)
        crossed = (user_wide * item_wide).astype(jnp.bfloat16)
        pre_one = (
            jnp.dot(item, weight_item, preferred_element_type=jnp.float32)
            + jnp.dot(crossed, weight_cross, preferred_element_type=jnp.float32)
            + user_part
        )
        sig_one = jax.nn.sigmoid(pre_one)
        hid_one = (pre_one * sig_one).astype(jnp.bfloat16)
        pre_two = jnp.dot(hid_one, second, preferred_element_type=jnp.float32) + bias_two_ref[...]
        sig_two = jax.nn.sigmoid(pre_two)
        hid_two = (pre_two * sig_two).astype(jnp.bfloat16)
        logits = jnp.sum(hid_two.astype(jnp.float32) * last, axis=1, keepdims=True)
        logit_grad = jax.nn.sigmoid(logits)
        if first == 0:
            place = lax.broadcasted_iota(jnp.int32, logits.shape, 0)
            logit_grad = logit_grad - jnp.where(place < users, 1.0, 0.0)
        logit_grad = loss_scale * logit_grad
        delta_two = (logit_grad * last * slope_of(pre_two, sig_two)).astype(jnp.bfloat16)
        delta_one = contract_last(delta_two, second) * slope_of(pre_one, sig_one)
        delta_one = delta_one.astype(jnp.bfloat16)
        back_cross = contract_last(delta_one, weight_cross)
        grads = contract_last(delta_one, weight_item) + back_cross * user_wide
        item_grads[first : first + PAIR_BLOCK, :] = grads.astype(jnp.bfloat16)
        delta_sum = delta_sum + fold(delta_one.astype(jnp.float32))
        cross_sum = cross_sum + fold(back_cross * item_wide)
    delta_high = delta_sum.astype(jnp.bfloat16)
    delta_low = (delta_sum - delta_high.astype(jnp.float32)).astype(jnp.bfloat16)
    user_grads = contract_last(delta_high, weight_user) + contract_last(delta_low, weight_user)
    user_out_ref[...] = (user_grads + cross_sum).astype(user_out_ref.dtype)
    index_row = row_ref[...]
    values = item_grads[...]
    for first in range(0, slots, ROW_BLOCK):
        store_tiles(sum_block(index_row, first, values), first, slot_ref)


def run_scorer(pair_slots, tiles, users, first_weight, first_bias, second_weight, second_bias, out_weight):
    pairs = pair_slots.size
    width = users.shape[1]
    by_column = pair_slots.T
    return pl.pallas_call(
        scorer_kernel,
        out_shape=(
            jax.ShapeDtypeStruct(tiles.shape, jnp.bfloat16),
            jax.ShapeDtypeStruct(users.shape, jnp.bfloat16),
        ),
        in_specs=[VMEM] * 9,
        out_specs=(VMEM, VMEM),
        scratch_shapes=[
            pltpu.VMEM((tiles.size // width, width), jnp.bfloat16),
            pltpu.VMEM((pairs, width), jnp.bfloat16),
        ],
        name="run_scorer",
        compiler_params=pltpu.CompilerParams(vmem_limit_bytes=24 << 20),
    )(
        by_column.reshape(pairs // 128, 128),
        by_column.reshape(1, pairs),
        tiles,
        users,
        first_weight,
        first_bias.reshape(1, -1),
        second_weight,
        second_bias.reshape(1, -1),
        out_weight.reshape(1, -1),
    )


def swap(blocks, axis):
    return lax.all_to_all(blocks, axis, split_axis=0, concat_axis=0, tiled=True)


def swap_tiles(tiles, count):
    return swap(tiles.reshape(count, -1, 128), BOTH).reshape(tiles.shape)


def body(
    node_table,
    user_vectors,
    first_weight,
    first_bias,
    second_weight,
    second_bias,
    out_weight,
    panel_rows,
    pair_slots,
):
    count_dp = lax.axis_size("dp")
    count_table = lax.axis_size("table")
    count = count_dp * count_table
    slot_cap = panel_rows.shape[2]
    wanted = panel_rows.reshape(count_dp, count_table, slot_cap).transpose(1, 0, 2)
    wanted = swap(wanted.reshape(count_table, count_dp * slot_cap), "table")
    wanted = wanted.reshape(count_table, count_dp, slot_cap).transpose(1, 0, 2)
    requested = swap(wanted.reshape(count_dp, count_table * slot_cap), "dp")
    panels = swap_tiles(pick_rows(requested, stage_table(node_table)), count)
    slot_grads, user_grads = run_scorer(
        pair_slots,
        panels,
        user_vectors,
        first_weight,
        first_bias,
        second_weight,
        second_bias,
        out_weight,
    )
    returned = swap_tiles(slot_grads, count)
    grad_table = sum_rows(requested.reshape(1, -1), returned, node_table.shape[0])
    return (grad_table, user_grads)


def solution(mesh):
    placed = (
        P(BOTH, None),
        P(BOTH, None),
        P(),
        P(),
        P(),
        P(),
        P(),
        P(BOTH, None, None),
        P(BOTH, None),
    )
    return jax.shard_map(
        body,
        mesh=mesh,
        in_specs=placed,
        out_specs=(P(BOTH, None), P(BOTH, None)),
        check_vma=False,
    )
```

```python
import jax
import jax.numpy as jnp
from jax import lax
from jax.experimental import pallas as pl
from jax.experimental.pallas import tpu as pltpu
from jax.sharding import PartitionSpec as P

loss_scale = 32.0
EACH = ("z", "core", "table")
PLANE = ("core", "table")
ROW_BLOCK = 512
PAIR_BLOCK = 512
PICK_BLOCK = 512


def slope_of(value, sig):
    return sig * (1.0 + value * (1.0 - sig))


def contract_last(left, right):
    return lax.dot_general(left, right, (((1,), (1,)), ((), ())), preferred_element_type=jnp.float32)


def low_half(rows):
    return lax.broadcasted_iota(jnp.int32, (rows, 8, 128), 1) < 4


def to_tiles(rows):
    groups = rows.shape[0] // 8
    parts = rows.reshape(groups, 8, 256)
    left, right = parts[:, :, :128], parts[:, :, 128:]
    low = low_half(groups)
    even = jnp.where(low, left, pltpu.roll(right, 4, 1))
    odd = jnp.where(low, pltpu.roll(left, 4, 1), right)
    return even, odd


def from_tiles(even, odd):
    groups = even.shape[0]
    low = low_half(groups)
    left = jnp.where(low, even, pltpu.roll(odd, 4, 1))
    right = jnp.where(low, pltpu.roll(even, 4, 1), odd)
    return left.reshape(groups * 8, 128), right.reshape(groups * 8, 128)


def unpack_tiles(tile_ref, out_ref):
    block = 64
    for first in range(0, tile_ref.shape[0], block):
        even = tile_ref[first : first + block, 0].astype(jnp.float32)
        odd = tile_ref[first : first + block, 1].astype(jnp.float32)
        left, right = from_tiles(even, odd)
        out_ref[8 * first : 8 * (first + block), :128] = left.astype(out_ref.dtype)
        out_ref[8 * first : 8 * (first + block), 128:] = right.astype(out_ref.dtype)


def store_tiles(rows, first, out_ref):
    even, odd = to_tiles(rows)
    at = first // 8
    out_ref[at : at + even.shape[0], 0] = even.astype(out_ref.dtype)
    out_ref[at : at + even.shape[0], 1] = odd.astype(out_ref.dtype)


def pick_block(columns, first, count, table):
    part = columns.shape[0]
    hot = []
    for at in range(first // part, (first + count) // part):
        ids = lax.broadcasted_iota(jnp.int32, (part, table.shape[0]), 1)
        hot.append((columns[:, at : at + 1] == ids).astype(jnp.float32).astype(jnp.bfloat16))
    return jnp.dot(jnp.concatenate(hot, axis=0), table, preferred_element_type=jnp.float32)


def sum_block(index_row, first, values):
    count = index_row.shape[1]
    row_id = lax.broadcasted_iota(jnp.int32, (ROW_BLOCK, count), 0) + first
    hot = (row_id == index_row).astype(jnp.float32).astype(jnp.bfloat16)
    return jnp.dot(hot, values, preferred_element_type=jnp.float32)


VMEM = pl.BlockSpec(memory_space=pltpu.VMEM)


def pick_kernel(index_ref, table_ref, out_ref):
    table = table_ref[...]
    columns = index_ref[...].T
    for first in range(0, index_ref.size, PICK_BLOCK):
        store_tiles(pick_block(columns, first, PICK_BLOCK, table), first, out_ref)


def pick_rows(index, table):
    return pl.pallas_call(
        pick_kernel,
        out_shape=jax.ShapeDtypeStruct((index.size // 8, 2, 8, 128), table.dtype),
        in_specs=[VMEM] * 2,
        out_specs=VMEM,
        name="pick_rows",
        compiler_params=pltpu.CompilerParams(
            vmem_limit_bytes=24 << 20
        ),
    )(index.reshape(-1, 128), table)


def sum_kernel(index_ref, tile_ref, out_ref, values):
    @pl.when(pl.program_id(0) == 0)
    def _():
        unpack_tiles(tile_ref, values)

    first = pl.program_id(0) * ROW_BLOCK
    out_ref[...] = sum_block(index_ref[...], first, values[...])


def sum_rows(index_row, tiles, rows):
    count = index_row.shape[1]
    return pl.pallas_call(
        sum_kernel,
        out_shape=jax.ShapeDtypeStruct((rows, 256), jnp.float32),
        grid=(rows // ROW_BLOCK,),
        in_specs=[
            pl.BlockSpec((1, count), lambda i: (0, 0)),
            pl.BlockSpec(tiles.shape, lambda i: (0, 0, 0, 0)),
        ],
        out_specs=pl.BlockSpec((ROW_BLOCK, 256), lambda i: (i, 0)),
        scratch_shapes=[pltpu.VMEM((count, 256), tiles.dtype)],
        name="sum_rows",
        compiler_params=pltpu.CompilerParams(vmem_limit_bytes=24 << 20),
    )(index_row, tiles)


def scorer_kernel(
    index_ref,
    row_ref,
    tile_ref,
    user_ref,
    first_ref,
    bias_one_ref,
    second_ref,
    bias_two_ref,
    last_ref,
    slot_ref,
    user_out_ref,
    panel_ref,
    item_grads,
):
    users, width = user_ref.shape
    pairs = index_ref.size
    slots = panel_ref.shape[0]
    unpack_tiles(tile_ref, panel_ref)
    panels = panel_ref[...]
    columns = index_ref[...].T
    user = user_ref[...]
    last = last_ref[...].astype(jnp.float32)
    second = second_ref[...]
    weight_user = first_ref[:width, :]
    weight_item = first_ref[width : 2 * width, :]
    weight_cross = first_ref[2 * width :, :]
    repeat = PAIR_BLOCK // users
    user_wide = jnp.concatenate([user.astype(jnp.float32)] * repeat, axis=0)
    user_part = jnp.dot(user, weight_user, preferred_element_type=jnp.float32) + bias_one_ref[...]
    user_part = jnp.concatenate([user_part] * repeat, axis=0)

    def fold(block):
        total = block[:users]
        for at in range(1, repeat):
            total = total + block[at * users : (at + 1) * users]
        return total

    delta_sum = jnp.zeros((users, width), jnp.float32)
    cross_sum = jnp.zeros((users, width), jnp.float32)
    ahead = pick_block(columns, 0, PAIR_BLOCK, panels)
    for first in range(0, pairs, PAIR_BLOCK):
        item_wide = ahead
        if first + PAIR_BLOCK < pairs:
            ahead = pick_block(columns, first + PAIR_BLOCK, PAIR_BLOCK, panels)
        item = item_wide.astype(jnp.bfloat16)
        crossed = (user_wide * item_wide).astype(jnp.bfloat16)
        pre_one = (
            jnp.dot(item, weight_item, preferred_element_type=jnp.float32)
            + jnp.dot(crossed, weight_cross, preferred_element_type=jnp.float32)
            + user_part
        )
        sig_one = jax.nn.sigmoid(pre_one)
        hid_one = (pre_one * sig_one).astype(jnp.bfloat16)
        pre_two = jnp.dot(hid_one, second, preferred_element_type=jnp.float32) + bias_two_ref[...]
        sig_two = jax.nn.sigmoid(pre_two)
        hid_two = (pre_two * sig_two).astype(jnp.bfloat16)
        logits = jnp.sum(hid_two.astype(jnp.float32) * last, axis=1, keepdims=True)
        logit_grad = jax.nn.sigmoid(logits)
        if first == 0:
            place = lax.broadcasted_iota(jnp.int32, logits.shape, 0)
            logit_grad = logit_grad - jnp.where(place < users, 1.0, 0.0)
        logit_grad = loss_scale * logit_grad
        delta_two = (logit_grad * last * slope_of(pre_two, sig_two)).astype(jnp.bfloat16)
        delta_one = contract_last(delta_two, second) * slope_of(pre_one, sig_one)
        delta_one = delta_one.astype(jnp.bfloat16)
        back_cross = contract_last(delta_one, weight_cross)
        grads = contract_last(delta_one, weight_item) + back_cross * user_wide
        item_grads[first : first + PAIR_BLOCK, :] = grads.astype(jnp.bfloat16)
        delta_sum = delta_sum + fold(delta_one.astype(jnp.float32))
        cross_sum = cross_sum + fold(back_cross * item_wide)
    delta_high = delta_sum.astype(jnp.bfloat16)
    delta_low = (delta_sum - delta_high.astype(jnp.float32)).astype(jnp.bfloat16)
    user_grads = contract_last(delta_high, weight_user) + contract_last(delta_low, weight_user)
    user_out_ref[...] = (user_grads + cross_sum).astype(user_out_ref.dtype)
    index_row = row_ref[...]
    values = item_grads[...]
    for first in range(0, slots, ROW_BLOCK):
        store_tiles(sum_block(index_row, first, values), first, slot_ref)


def run_scorer(pair_slots, tiles, users, first_weight, first_bias, second_weight, second_bias, out_weight):
    pairs = pair_slots.size
    width = users.shape[1]
    by_column = pair_slots.T
    return pl.pallas_call(
        scorer_kernel,
        out_shape=(
            jax.ShapeDtypeStruct(tiles.shape, jnp.bfloat16),
            jax.ShapeDtypeStruct(users.shape, jnp.bfloat16),
        ),
        in_specs=[VMEM] * 9,
        out_specs=(VMEM, VMEM),
        scratch_shapes=[
            pltpu.VMEM((tiles.size // width, width), jnp.bfloat16),
            pltpu.VMEM((pairs, width), jnp.bfloat16),
        ],
        name="run_scorer",
        compiler_params=pltpu.CompilerParams(vmem_limit_bytes=24 << 20),
    )(
        by_column.reshape(pairs // 128, 128),
        by_column.reshape(1, pairs),
        tiles,
        users,
        first_weight,
        first_bias.reshape(1, -1),
        second_weight,
        second_bias.reshape(1, -1),
        out_weight.reshape(1, -1),
    )


def swap(blocks, axis):
    return lax.all_to_all(blocks, axis, split_axis=0, concat_axis=0, tiled=True)


def swap_tiles(tiles, count):
    return swap(tiles.reshape(count, -1, 128), EACH).reshape(tiles.shape)


def body(
    node_table,
    user_vectors,
    first_weight,
    first_bias,
    second_weight,
    second_bias,
    out_weight,
    panel_rows,
    pair_slots,
):
    count_z = lax.axis_size("z")
    count_plane = lax.axis_size(PLANE)
    count = count_z * count_plane
    slot_cap = panel_rows.shape[2]
    wanted = panel_rows.reshape(count_z, count_plane, slot_cap).transpose(1, 0, 2)
    wanted = swap(wanted.reshape(count_plane, count_z * slot_cap), PLANE)
    wanted = wanted.reshape(count_plane, count_z, slot_cap).transpose(1, 0, 2)
    requested = swap(wanted.reshape(count_z, count_plane * slot_cap), "z")
    panels = swap_tiles(pick_rows(requested, node_table), count)
    slot_grads, user_grads = run_scorer(
        pair_slots,
        panels,
        user_vectors,
        first_weight,
        first_bias,
        second_weight,
        second_bias,
        out_weight,
    )
    returned = swap_tiles(slot_grads, count)
    grad_table = sum_rows(requested.reshape(1, -1), returned, node_table.shape[0])
    return (grad_table, user_grads)


def solution(mesh):
    cores = 2
    shape = (mesh.shape["dp"] // cores, cores, mesh.shape["table"])
    fine = jax.sharding.Mesh(mesh.devices.reshape(shape), EACH)
    placed = (
        P(EACH, None),
        P(EACH, None),
        P(),
        P(),
        P(),
        P(),
        P(),
        P(EACH, None, None),
        P(EACH, None),
    )
    return jax.shard_map(
        body,
        mesh=fine,
        in_specs=placed,
        out_specs=(P(EACH, None), P(EACH, None)),
        check_vma=False,
    )
```

```python
import jax
import jax.numpy as jnp
from jax import lax
from jax.experimental import pallas as pl
from jax.experimental.pallas import tpu as pltpu
from jax.sharding import PartitionSpec as P

loss_scale = 32.0
EACH = ("z", "core", "table")
PLANE = ("core", "table")
ROW_BLOCK = 512
PAIR_BLOCK = 512
PICK_BLOCK = 512


def slope_of(value, sig):
    return sig * (1.0 + value * (1.0 - sig))


def contract_last(left, right):
    return lax.dot_general(left, right, (((1,), (1,)), ((), ())), preferred_element_type=jnp.float32)


def low_half(rows):
    return lax.broadcasted_iota(jnp.int32, (rows, 8, 128), 1) < 4


def to_tiles(rows):
    groups = rows.shape[0] // 8
    parts = rows.reshape(groups, 8, 256)
    left, right = parts[:, :, :128], parts[:, :, 128:]
    low = low_half(groups)
    even = jnp.where(low, left, pltpu.roll(right, 4, 1))
    odd = jnp.where(low, pltpu.roll(left, 4, 1), right)
    return even, odd


def from_tiles(even, odd):
    groups = even.shape[0]
    low = low_half(groups)
    left = jnp.where(low, even, pltpu.roll(odd, 4, 1))
    right = jnp.where(low, pltpu.roll(even, 4, 1), odd)
    return left.reshape(groups * 8, 128), right.reshape(groups * 8, 128)


def unpack_tiles(tile_ref, out_ref):
    block = 64
    for first in range(0, tile_ref.shape[0], block):
        even = tile_ref[first : first + block, 0].astype(jnp.float32)
        odd = tile_ref[first : first + block, 1].astype(jnp.float32)
        left, right = from_tiles(even, odd)
        out_ref[8 * first : 8 * (first + block), :128] = left.astype(out_ref.dtype)
        out_ref[8 * first : 8 * (first + block), 128:] = right.astype(out_ref.dtype)


def store_tiles(rows, first, out_ref):
    even, odd = to_tiles(rows)
    at = first // 8
    out_ref[at : at + even.shape[0], 0] = even.astype(out_ref.dtype)
    out_ref[at : at + even.shape[0], 1] = odd.astype(out_ref.dtype)


def pick_block(columns, first, count, table):
    part = columns.shape[0]
    hot = []
    for at in range(first // part, (first + count) // part):
        ids = lax.broadcasted_iota(jnp.int32, (part, table.shape[0]), 1)
        hot.append((columns[:, at : at + 1] == ids).astype(jnp.float32).astype(jnp.bfloat16))
    return jnp.dot(jnp.concatenate(hot, axis=0), table, preferred_element_type=jnp.float32)


def sum_block(index_row, first, values):
    count = index_row.shape[1]
    row_id = lax.broadcasted_iota(jnp.int32, (ROW_BLOCK, count), 0) + first
    hot = (row_id == index_row).astype(jnp.float32).astype(jnp.bfloat16)
    return jnp.dot(hot, values, preferred_element_type=jnp.float32)


VMEM = pl.BlockSpec(memory_space=pltpu.VMEM)


ANYWHERE = pl.BlockSpec(memory_space=pl.ANY)


def send_block(staged, out_ref, sems, at, count):
    rows = pl.ds(at * count, count)
    copy = pltpu.make_async_copy(staged.at[rows], out_ref.at[rows], sems.at[at])
    copy.start()
    return copy


def pick_kernel(index_ref, table_ref, out_ref, staged, sems):
    table = table_ref[...]
    columns = index_ref[...].T
    copies = []
    for at in range(index_ref.size // PICK_BLOCK):
        first = at * PICK_BLOCK
        store_tiles(pick_block(columns, first, PICK_BLOCK, table), first, staged)
        copies.append(send_block(staged, out_ref, sems, at, PICK_BLOCK // 8))
    for copy in copies:
        copy.wait()


def pick_rows(index, table):
    shape = (index.size // 8, 2, 8, 128)
    return pl.pallas_call(
        pick_kernel,
        out_shape=jax.ShapeDtypeStruct(shape, table.dtype),
        in_specs=[VMEM] * 2,
        out_specs=ANYWHERE,
        scratch_shapes=[
            pltpu.VMEM(shape, table.dtype),
            pltpu.SemaphoreType.DMA((index.size // PICK_BLOCK,)),
        ],
        name="pick_rows",
        compiler_params=pltpu.CompilerParams(
            vmem_limit_bytes=24 << 20
        ),
    )(index.reshape(-1, 128), table)


def sum_kernel(index_ref, tile_ref, out_ref, values_ref, staged, sems):
    unpack_tiles(tile_ref, values_ref)
    index_row = index_ref[...]
    values = values_ref[...]
    copies = []
    for at in range(out_ref.shape[0] // ROW_BLOCK):
        first = at * ROW_BLOCK
        staged[first : first + ROW_BLOCK, :] = sum_block(index_row, first, values)
        copies.append(send_block(staged, out_ref, sems, at, ROW_BLOCK))
    for copy in copies:
        copy.wait()


def sum_rows(index_row, tiles, rows):
    count = index_row.shape[1]
    return pl.pallas_call(
        sum_kernel,
        out_shape=jax.ShapeDtypeStruct((rows, 256), jnp.float32),
        in_specs=[VMEM] * 2,
        out_specs=ANYWHERE,
        scratch_shapes=[
            pltpu.VMEM((count, 256), tiles.dtype),
            pltpu.VMEM((rows, 256), jnp.float32),
            pltpu.SemaphoreType.DMA((rows // ROW_BLOCK,)),
        ],
        name="sum_rows",
        compiler_params=pltpu.CompilerParams(vmem_limit_bytes=24 << 20),
    )(index_row, tiles)


def scorer_kernel(
    index_ref,
    row_ref,
    tile_ref,
    user_ref,
    first_ref,
    bias_one_ref,
    second_ref,
    bias_two_ref,
    last_ref,
    slot_ref,
    user_out_ref,
    panel_ref,
    item_grads,
):
    users, width = user_ref.shape
    pairs = index_ref.size
    slots = panel_ref.shape[0]
    unpack_tiles(tile_ref, panel_ref)
    panels = panel_ref[...]
    columns = index_ref[...].T
    user = user_ref[...]
    last = last_ref[...].astype(jnp.float32)
    second = second_ref[...]
    weight_user = first_ref[:width, :]
    weight_item = first_ref[width : 2 * width, :]
    weight_cross = first_ref[2 * width :, :]
    repeat = PAIR_BLOCK // users
    user_wide = jnp.concatenate([user.astype(jnp.float32)] * repeat, axis=0)
    user_part = jnp.dot(user, weight_user, preferred_element_type=jnp.float32) + bias_one_ref[...]
    user_part = jnp.concatenate([user_part] * repeat, axis=0)

    def fold(block):
        total = block[:users]
        for at in range(1, repeat):
            total = total + block[at * users : (at + 1) * users]
        return total

    delta_sum = jnp.zeros((users, width), jnp.float32)
    cross_sum = jnp.zeros((users, width), jnp.float32)
    ahead = pick_block(columns, 0, PAIR_BLOCK, panels)
    for first in range(0, pairs, PAIR_BLOCK):
        item_wide = ahead
        if first + PAIR_BLOCK < pairs:
            ahead = pick_block(columns, first + PAIR_BLOCK, PAIR_BLOCK, panels)
        item = item_wide.astype(jnp.bfloat16)
        crossed = (user_wide * item_wide).astype(jnp.bfloat16)
        pre_one = (
            jnp.dot(item, weight_item, preferred_element_type=jnp.float32)
            + jnp.dot(crossed, weight_cross, preferred_element_type=jnp.float32)
            + user_part
        )
        sig_one = jax.nn.sigmoid(pre_one)
        hid_one = (pre_one * sig_one).astype(jnp.bfloat16)
        pre_two = jnp.dot(hid_one, second, preferred_element_type=jnp.float32) + bias_two_ref[...]
        sig_two = jax.nn.sigmoid(pre_two)
        hid_two = (pre_two * sig_two).astype(jnp.bfloat16)
        logits = jnp.sum(hid_two.astype(jnp.float32) * last, axis=1, keepdims=True)
        logit_grad = jax.nn.sigmoid(logits)
        if first == 0:
            place = lax.broadcasted_iota(jnp.int32, logits.shape, 0)
            logit_grad = logit_grad - jnp.where(place < users, 1.0, 0.0)
        logit_grad = loss_scale * logit_grad
        delta_two = (logit_grad * last * slope_of(pre_two, sig_two)).astype(jnp.bfloat16)
        delta_one = contract_last(delta_two, second) * slope_of(pre_one, sig_one)
        delta_one = delta_one.astype(jnp.bfloat16)
        back_cross = contract_last(delta_one, weight_cross)
        grads = contract_last(delta_one, weight_item) + back_cross * user_wide
        item_grads[first : first + PAIR_BLOCK, :] = grads.astype(jnp.bfloat16)
        delta_sum = delta_sum + fold(delta_one.astype(jnp.float32))
        cross_sum = cross_sum + fold(back_cross * item_wide)
    delta_high = delta_sum.astype(jnp.bfloat16)
    delta_low = (delta_sum - delta_high.astype(jnp.float32)).astype(jnp.bfloat16)
    user_grads = contract_last(delta_high, weight_user) + contract_last(delta_low, weight_user)
    user_out_ref[...] = (user_grads + cross_sum).astype(user_out_ref.dtype)
    index_row = row_ref[...]
    values = item_grads[...]
    for first in range(0, slots, ROW_BLOCK):
        store_tiles(sum_block(index_row, first, values), first, slot_ref)


def run_scorer(pair_slots, tiles, users, first_weight, first_bias, second_weight, second_bias, out_weight):
    pairs = pair_slots.size
    width = users.shape[1]
    by_column = pair_slots.T
    return pl.pallas_call(
        scorer_kernel,
        out_shape=(
            jax.ShapeDtypeStruct(tiles.shape, jnp.bfloat16),
            jax.ShapeDtypeStruct(users.shape, jnp.bfloat16),
        ),
        in_specs=[VMEM] * 9,
        out_specs=(VMEM, VMEM),
        scratch_shapes=[
            pltpu.VMEM((tiles.size // width, width), jnp.bfloat16),
            pltpu.VMEM((pairs, width), jnp.bfloat16),
        ],
        name="run_scorer",
        compiler_params=pltpu.CompilerParams(vmem_limit_bytes=24 << 20),
    )(
        by_column.reshape(pairs // 128, 128),
        by_column.reshape(1, pairs),
        tiles,
        users,
        first_weight,
        first_bias.reshape(1, -1),
        second_weight,
        second_bias.reshape(1, -1),
        out_weight.reshape(1, -1),
    )


def swap(blocks, axis):
    return lax.all_to_all(blocks, axis, split_axis=0, concat_axis=0, tiled=True)


def swap_tiles(tiles, count):
    return swap(tiles.reshape(count, -1, 128), EACH).reshape(tiles.shape)


def body(
    node_table,
    user_vectors,
    first_weight,
    first_bias,
    second_weight,
    second_bias,
    out_weight,
    panel_rows,
    pair_slots,
):
    count_z = lax.axis_size("z")
    count_plane = lax.axis_size(PLANE)
    count = count_z * count_plane
    slot_cap = panel_rows.shape[2]
    wanted = panel_rows.reshape(count_z, count_plane, slot_cap).transpose(1, 0, 2)
    wanted = swap(wanted.reshape(count_plane, count_z * slot_cap), PLANE)
    wanted = wanted.reshape(count_plane, count_z, slot_cap).transpose(1, 0, 2)
    requested = swap(wanted.reshape(count_z, count_plane * slot_cap), "z")
    panels = swap_tiles(pick_rows(requested, node_table), count)
    slot_grads, user_grads = run_scorer(
        pair_slots,
        panels,
        user_vectors,
        first_weight,
        first_bias,
        second_weight,
        second_bias,
        out_weight,
    )
    returned = swap_tiles(slot_grads, count)
    grad_table = sum_rows(requested.reshape(1, -1), returned, node_table.shape[0])
    return (grad_table, user_grads)


def solution(mesh):
    cores = 2
    shape = (mesh.shape["dp"] // cores, cores, mesh.shape["table"])
    fine = jax.sharding.Mesh(mesh.devices.reshape(shape), EACH)
    placed = (
        P(EACH, None),
        P(EACH, None),
        P(),
        P(),
        P(),
        P(),
        P(),
        P(EACH, None, None),
        P(EACH, None),
    )
    return jax.shard_map(
        body,
        mesh=fine,
        in_specs=placed,
        out_specs=(P(EACH, None), P(EACH, None)),
        check_vma=False,
    )
```
